32 devices in a mesh: blk: 4 (over z), head: 2 (over core), clip: 4 (over y, x).
Axes of the slice: x: 2, y: 2, z: 4, core: 2. Of those that a mesh axis runs over, the one named last changes fastest.
Arguments:
- tokens: bfloat16 [4608, 1536], P(('clip', 'blk', 'head')), parts along dimension 0, may hold values from -6 to 6
- modulation: float32 [12, 1536], P('clip'), parts along dimension 0, may hold values from -3 to 3
- w_qkv: bfloat16 [1536, 3, 1536], P(None, None, 'head'), may hold values from -0.25 to 0.25
- w_out: bfloat16 [1536, 1536], P('head'), may hold values from -0.15625 to 0.15625
- w_cross: bfloat16 [1536, 1536], P(None, 'head'), may hold values from -0.15625 to 0.15625
- q_gain: float32 [128], replicated, may hold values from 0.5 to 6
- k_gain: float32 [128], replicated, may hold values from 0.5 to 6
- cross_gain: float32 [128], replicated, may hold values from 0.5 to 6
- scene_keys: bfloat16 [1024, 1536], P(('clip', 'blk'), 'head'), parts along dimension 0, may hold values from -40 to 40
- scene_values: bfloat16 [1024, 1536], P(('clip', 'blk'), 'head'), parts along dimension 0, may hold values from -6 to 6
Outputs:
- hidden: bfloat16 [4608, 1536], P(('clip', 'blk', 'head')), parts along dimension 0
- cross_context: bfloat16 [4608, 1536], P(('clip', 'blk'), 'head'), parts along dimension 0
The draws below stay inside these ranges and needn't reach their ends.
There are 4 independent parts, one for each index of `clip`. The reference program is written for one: setup_inputs(seed, part) draws one part's arguments, and reference() takes and returns one part's arrays. A program takes and returns all parts, laid end to end along the dimension named above; an argument that names none is the same for every part. Nothing has to cross between parts.
All inputs are finite; a program needn't handle non-finite values.
Results may differ from the reference program's by a relative error of at most 0.015.
The reference program's roundings to bfloat16 on the way (of `modulated`, `context` and `cross_queries`) count: a program that leaves them out, or rounds other values in their place, can miss the bound.
Values may be sent and summed in bfloat16 or wider, within the bound.
No kernel may reach another device: no remote copies, remote signals or barrier semaphores. Data moves between devices by JAX's collectives and lax.ppermute only.
A program may use at most 128 MiB of HBM per device.

```python
import jax
import jax.numpy as jnp
from jax import lax

D = 1536
HEADS = 12
HD = 128
S = 1152
SC = 256


def draw_tokens(key, part):
    base = jax.random.normal(key, (S, D), jnp.float32)
    return jnp.clip(base, -6.0, 6.0).astype(jnp.bfloat16)


def draw_w_qkv(key, part):
    base = jax.random.normal(key, (D, 3, D), jnp.float32) / D ** 0.5
    return jnp.clip(base, -0.25, 0.25).astype(jnp.bfloat16)


def gain_common(key, salt):
    own_key = jax.random.fold_in(key, salt)
    return jnp.exp(jax.random.uniform(own_key, (HD,), jnp.float32, 0.26, 0.83))


def draw_q_gain(key, part):
    return gain_common(key, 1)


def draw_k_gain(key, part):
    return gain_common(key, 2)


def draw_cross_gain(key, part):
    return gain_common(key, 3)


def draw_scene_keys(key, part):
    base = jax.random.normal(key, (SC, D), jnp.float32)
    return jnp.clip(base, -40.0, 40.0).astype(jnp.bfloat16)


def levels(rng, extent, pieces, least, top_value):
    level = 1.0
    for axis_at, shards_of in pieces:
        steps = jax.random.uniform(jax.random.fold_in(jax.random.fold_in(rng, 6), axis_at), (shards_of,), jnp.float32, least / len(pieces), top_value / len(pieces))
        level = level * jnp.repeat(jnp.exp(steps), extent[axis_at] // shards_of).reshape((-1,) + (1,) * (len(extent) - 1 - axis_at))
    return level


def scatter_about(stream_key, dims, scale, bound, cuts=(), held_as=jnp.bfloat16):
    values = jax.random.normal(stream_key, dims, jnp.float32) * scale
    if len(cuts) > 0:
        values = levels(stream_key, dims, cuts, -0.22, 0.18) * values
    return jnp.clip(values, min=-bound, max=bound).astype(held_as)


def setup_inputs(seed: int = 0, part: int = 0) -> dict:
    arg_keys = jax.random.split(jax.random.key(seed), 11)
    own_keys = jax.random.split(jax.random.fold_in(arg_keys[10], part), 11)
    return {
        "tokens": draw_tokens(jax.random.fold_in(jax.random.fold_in(arg_keys[10], part), 71), part),
        "modulation": scatter_about(own_keys[1], (3, D), 0.5, 3.0, (), jnp.float32),
        "w_qkv": draw_w_qkv(jax.random.fold_in(arg_keys[10], 71), part),
        "w_out": scatter_about(arg_keys[3], (D, D), D ** -0.5, 0.15625, ((0, 2),)),
        "w_cross": scatter_about(arg_keys[4], (D, D), D ** -0.5, 0.15625, ((1, 2),)),
        "q_gain": draw_q_gain(jax.random.fold_in(arg_keys[10], 71), part),
        "k_gain": draw_k_gain(jax.random.fold_in(arg_keys[10], 71), part),
        "cross_gain": draw_cross_gain(jax.random.fold_in(arg_keys[10], 71), part),
        "scene_keys": draw_scene_keys(jax.random.fold_in(jax.random.fold_in(arg_keys[10], part), 71), part),
        "scene_values": scatter_about(own_keys[9], (SC, D), 1.0, 6.0, ((0, 4), (1, 2))),
    }


def head_norm(values, gain):
    rms = lax.optimization_barrier(jnp.mean(values * values, axis=-1, keepdims=True))
    return values * lax.rsqrt(rms + 1e-06) * gain

def attention(queries, keys_all, values_all):
    rows = queries.shape[0]
    block = 512 if rows % 512 == 0 else rows
    scale = 1.0 / HD ** 0.5
    keys_f = keys_all.astype(jnp.float32)
    values_f = values_all.astype(jnp.float32)

    def one_block(query_blk):
        scores = jnp.einsum('rhd,nhd->hrn', query_blk.astype(jnp.float32), keys_f) * scale
        probs = jax.nn.softmax(scores, axis=-1)
        return jnp.einsum('hrn,nhd->rhd', probs, values_f)
    blocks = queries.reshape(rows // block, block, HEADS, HD)
    result = lax.map(one_block, blocks)
    return result.reshape(rows, D)

def reference(tokens, modulation, w_qkv, w_out, w_cross, q_gain, k_gain, cross_gain, scene_keys, scene_values):
    xfloat = tokens.astype(jnp.float32)
    mean = lax.optimization_barrier(jnp.mean(xfloat, axis=-1, keepdims=True))
    var = lax.optimization_barrier(jnp.mean((xfloat - mean) ** 2, axis=-1, keepdims=True))
    normed = (xfloat - mean) * lax.rsqrt(var + 1e-06)
    modulated = (normed * (1.0 + modulation[1]) + modulation[0]).astype(jnp.bfloat16)
    projected = jnp.dot(modulated, w_qkv.reshape(D, 3 * D), preferred_element_type=jnp.float32)
    projected = projected.reshape(S, 3, HEADS, HD)
    queries = head_norm(projected[:, 0], q_gain).astype(jnp.bfloat16)
    keys_n = head_norm(projected[:, 1], k_gain).astype(jnp.bfloat16)
    values = projected[:, 2].astype(jnp.bfloat16)
    context = attention(queries, keys_n, values).astype(jnp.bfloat16)
    attn = jnp.dot(context, w_out, preferred_element_type=jnp.float32)
    hidden = (xfloat + modulation[2] * attn).astype(jnp.bfloat16)
    cross_proj = jnp.dot(hidden, w_cross, preferred_element_type=jnp.float32).reshape(S, HEADS, HD)
    cross_queries = head_norm(cross_proj, cross_gain).astype(jnp.bfloat16)
    cross_context = attention(cross_queries, scene_keys.reshape(SC, HEADS, HD), scene_values.reshape(SC, HEADS, HD))
    return (hidden, cross_context.astype(jnp.bfloat16))
```

```python
import functools
import math

import jax
import jax.numpy as jnp
from jax import lax
from jax.experimental import pallas as pl
from jax.experimental.pallas import tpu as pltpu
from jax.sharding import PartitionSpec as P

HD = 128
EPS = 1e-06


def modulate(rows, mod_ref):
    xfloat = rows.astype(jnp.float32)
    mean = jnp.mean(xfloat, axis=-1, keepdims=True)
    centred = xfloat - mean
    var = jnp.mean(centred * centred, axis=-1, keepdims=True)
    normed = centred * lax.rsqrt(var + EPS)
    return (normed * (1.0 + mod_ref[1:2, :]) + mod_ref[0:1, :]).astype(jnp.bfloat16)


def head_norm(values, gain):
    rms = jnp.mean(values * values, axis=-1, keepdims=True)
    return (values * lax.rsqrt(rms + EPS) * gain).astype(jnp.bfloat16)


def dot(left, right):
    return jnp.dot(left, right, preferred_element_type=jnp.float32)


def dot_t(left, right):
    return lax.dot_general(
        left, right, (((1,), (1,)), ((), ())), preferred_element_type=jnp.float32
    )


def column_step(width):
    return 2 * HD if width % (2 * HD) == 0 else HD


def blocks_kernel(n_rows, first, last, scale, *refs):
    refs = list(refs)
    row_refs = [refs.pop(0) for _ in range(n_rows)]
    mod_ref, w_ref, kg_ref = refs.pop(0), refs.pop(0), refs.pop(0)
    if first:
        qg_ref = refs.pop(0)
    else:
        q_ref, state_in, acc_in = refs.pop(0), refs.pop(0), refs.pop(0)
    if last:
        ctx_ref = refs.pop(0)
    else:
        if first:
            q_ref = refs.pop(0)
        state_out, acc_out = refs.pop(0), refs.pop(0)
    rows_ref = refs.pop(0)
    at = 0
    for ref in row_refs:
        count = ref.shape[0]
        rows_ref[at : at + count, :] = modulate(ref[...], mod_ref)
        at += count
    width = w_ref.shape[2]
    wide = column_step(width)
    rows = rows_ref[...]
    for c in range(0, width, wide):
        if first:
            q_wide = dot(rows, w_ref[0, :, c : c + wide])
        k_wide = dot(rows, w_ref[1, :, c : c + wide])
        v_wide = dot(rows, w_ref[2, :, c : c + wide]).astype(jnp.bfloat16)
        for j in range(0, wide, HD):
            h = (c + j) // HD
            lanes = slice(c + j, c + j + HD)
            keys = head_norm(k_wide[:, j : j + HD], kg_ref[...])
            values = v_wide[:, j : j + HD]
            if first:
                queries = head_norm(q_wide[:, j : j + HD], qg_ref[...])
                q_ref[:, lanes] = queries
            else:
                queries = q_ref[:, lanes]
            scores = dot_t(queries, keys)
            best = jnp.max(scores, axis=-1, keepdims=True)
            if not first:
                before = state_in[:, 2 * h : 2 * h + 1]
                best = jnp.maximum(best, before)
            weights = jnp.exp((scores - best) * scale)
            total = jnp.sum(weights, axis=-1, keepdims=True)
            accum = dot(weights.astype(jnp.bfloat16), values)
            if not first:
                factor = jnp.exp((before - best) * scale)
                total = total + factor * state_in[:, 2 * h + 1 : 2 * h + 2]
                accum = accum + factor * acc_in[:, lanes]
            if last:
                ctx_ref[:, lanes] = (accum / total).astype(jnp.bfloat16)
            else:
                state_out[:, 2 * h : 2 * h + 1] = best
                state_out[:, 2 * h + 1 : 2 * h + 2] = total
                acc_out[:, lanes] = accum


def final_kernel(
    n_scene, scale,
    me_ref, ctx_ref, ctx_p_ref, own_ref, other_ref, mod_ref, wo_ref, wo_p_ref, wc_ref, cg_ref, *refs
):
    scene_refs = refs[:n_scene]
    hidden_ref, out_ref, hid_ref, keys_ref = refs[n_scene:]
    half = own_ref.shape[0]
    width = ctx_ref.shape[1]
    model = own_ref.shape[1]
    wide = column_step(width)
    swapped = jnp.concatenate([ctx_p_ref[half:, :], ctx_p_ref[:half, :]], axis=0)
    mine = ctx_ref[...]
    for c in range(0, model, wide):
        cols = slice(c, c + wide)
        attn = dot(mine, wo_ref[:, cols]) + dot(swapped, wo_p_ref[:, cols])
        gated = mod_ref[2:3, cols] * attn
        own = (own_ref[:, cols].astype(jnp.float32) + gated[:half]).astype(jnp.bfloat16)
        hidden_ref[:, cols] = own
        hid_ref[:half, cols] = own
        hid_ref[half:, cols] = (
            other_ref[:, cols].astype(jnp.float32) + gated[half:]
        ).astype(jnp.bfloat16)
    each = scene_refs[0].shape[0] // 2
    for i, ref in enumerate(scene_refs):
        keys_ref[0, i * each : (i + 1) * each, :] = ref[:each, :]
        keys_ref[1, i * each : (i + 1) * each, :] = ref[each:, :]
    rows = hid_ref[...]
    me = me_ref[0]
    at_own = pl.multiple_of(me * half, half)
    at_other = pl.multiple_of((1 - me) * half, half)
    for c in range(0, width, wide):
        q_wide = dot(rows, wc_ref[:, c : c + wide])
        for j in range(0, wide, HD):
            lanes = slice(c + j, c + j + HD)
            queries = head_norm(q_wide[:, j : j + HD], cg_ref[...])
            scores = dot_t(queries, keys_ref[0, :, lanes])
            best = jnp.max(scores, axis=-1, keepdims=True)
            weights = jnp.exp((scores - best) * scale)
            total = jnp.sum(weights, axis=-1, keepdims=True)
            accum = dot(weights.astype(jnp.bfloat16), keys_ref[1, :, lanes])
            result = (accum / total).astype(jnp.bfloat16)
            out_ref[pl.ds(at_own, half), lanes] = result[:half]
            out_ref[pl.ds(at_other, half), lanes] = result[half:]


VM = pl.BlockSpec(memory_space=pltpu.VMEM)
SM = pl.BlockSpec(memory_space=pltpu.SMEM)
PARAMS = pltpu.CompilerParams(vmem_limit_bytes=48 * 1024 * 1024)


def blocks_call(row_list, mod, w3, q_gain, k_gain, carry, last, name):
    first = carry is None
    model = row_list[0].shape[1]
    keys = sum(r.shape[0] for r in row_list)
    width = w3.shape[2]
    rows_q = keys if first else carry[0].shape[0]
    args = list(row_list) + [mod, w3, k_gain]
    args += [q_gain] if first else list(carry)
    shapes = []
    if last:
        shapes.append(jax.ShapeDtypeStruct((rows_q, width), jnp.bfloat16))
    else:
        if first:
            shapes.append(jax.ShapeDtypeStruct((rows_q, width), jnp.bfloat16))
        shapes.append(jax.ShapeDtypeStruct((rows_q, HD), jnp.float32))
        shapes.append(jax.ShapeDtypeStruct((rows_q, width), jnp.float32))
    flops = 2 * keys * model * width * (3 if first else 2) + 4 * rows_q * keys * width
    out = pl.pallas_call(
        functools.partial(
            blocks_kernel, len(row_list), first, last, 1.0 / math.sqrt(HD)
        ),
        out_shape=shapes,
        in_specs=[VM] * len(args),
        out_specs=[VM] * len(shapes),
        scratch_shapes=[pltpu.VMEM((keys, model), jnp.bfloat16)],
        compiler_params=PARAMS,
        cost_estimate=pl.CostEstimate(
            flops=flops,
            transcendentals=rows_q * keys * width // HD,
            bytes_accessed=2 * keys * model + 6 * model * width,
        ),
        name=name,
    )(*args)
    if last:
        return out[0]
    return tuple(out) if first else (carry[0],) + tuple(out)


def final_call(me, ctx, ctx_p, own, other, mod, wo, wo_p, wc, cg, scenes):
    half, model = own.shape
    rows, width = ctx.shape
    each = scenes[0].shape[0] // 2
    args = [me, ctx, ctx_p, own, other, mod, wo, wo_p, wc, cg] + list(scenes)
    flops = 4 * rows * model * width + 2 * rows * model * width
    return pl.pallas_call(
        functools.partial(final_kernel, len(scenes), 1.0 / math.sqrt(HD)),
        out_shape=[
            jax.ShapeDtypeStruct((half, model), jnp.bfloat16),
            jax.ShapeDtypeStruct((rows, width), jnp.bfloat16),
        ],
        in_specs=[SM] + [VM] * (len(args) - 1),
        out_specs=[VM, VM],
        scratch_shapes=[
            pltpu.VMEM((rows, model), jnp.bfloat16),
            pltpu.VMEM((2, each * len(scenes), width), jnp.bfloat16),
        ],
        compiler_params=PARAMS,
        cost_estimate=pl.CostEstimate(
            flops=flops,
            transcendentals=rows * each * len(scenes) * width // HD,
            bytes_accessed=6 * model * width,
        ),
        name="final",
    )(*args)


def swap_cores(x):
    return lax.ppermute(x, "head", [(0, 1), (1, 0)])


def shards(
    tokens, modulation, w_qkv, w_out, w_cross, q_gain, k_gain, cross_gain, scene_keys, scene_values
):
    count = lax.axis_size("blk")
    me = lax.axis_index("head").astype(jnp.int32).reshape(1)
    place = lax.axis_index("blk")
    w3 = jnp.transpose(w_qkv, (1, 0, 2))
    q_gain, k_gain, cross_gain = (g.reshape(1, HD) for g in (q_gain, k_gain, cross_gain))
    scene = jnp.concatenate([scene_keys, scene_values], axis=0)
    other = swap_cores(tokens)
    w_out_p = swap_cores(w_out)
    if count == 4:
        xor1 = [(i, i ^ 1) for i in range(4)]
        xor2 = [(i, i ^ 2) for i in range(4)]
        inner = [(1, 2), (2, 1)]
        outer = [(1, 0), (2, 3)]
        at_end = (place == 0) | (place == count - 1)

        def gather(x):
            near = lax.ppermute(x, "blk", xor1)
            far = lax.ppermute(x, "blk", xor2)
            mid = lax.ppermute(x, "blk", inner)
            out = lax.ppermute(far, "blk", outer)
            return [near, far, jnp.where(at_end, out, mid)]
    else:

        def gather(x):
            return [
                lax.ppermute(x, "blk", [(i, (i + s) % count) for i in range(count)])
                for s in range(1, count)
            ]

    slots = gather(tokens)
    scenes = [scene] + gather(scene)
    pairs = [(x, swap_cores(x)) for x in slots]
    carry = blocks_call(
        [tokens, other], modulation, w3, q_gain, k_gain, None, count == 1, "own"
    )
    while pairs:
        taken, pairs = (pairs[:2], pairs[2:]) if len(pairs) > 1 else (pairs, [])
        carry = blocks_call(
            [r for pair in taken for r in pair],
            modulation, w3, q_gain, k_gain, carry, not pairs, "more" if pairs else "last",
        )
    ctx = carry
    ctx_p = swap_cores(ctx)
    hidden, cross_context = final_call(
        me, ctx, ctx_p, tokens, other, modulation, w_out, w_out_p, w_cross, cross_gain, scenes
    )
    return (hidden, cross_context)


def solution(mesh):
    return jax.shard_map(
        shards,
        mesh=mesh,
        in_specs=(
            P(("clip", "blk", "head"), None),
            P("clip", None),
            P(None, None, "head"),
            P("head", None),
            P(None, "head"),
            P(),
            P(),
            P(),
            P(("clip", "blk"), "head"),
            P(("clip", "blk"), "head"),
        ),
        out_specs=(P(("clip", "blk", "head"), None), P(("clip", "blk"), "head")),
        check_vma=False,
    )
```

```python
import functools
import math

import jax
import jax.numpy as jnp
from jax import lax
from jax.experimental import pallas as pl
from jax.experimental.pallas import tpu as pltpu
from jax.sharding import PartitionSpec as P


HD = 128
EPS = 1e-06


def modulate(rows, shift, scale):
    xfloat = rows.astype(jnp.float32)
    mean = jnp.mean(xfloat, axis=-1, keepdims=True)
    centred = xfloat - mean
    var = jnp.mean(centred * centred, axis=-1, keepdims=True)
    normed = centred * lax.rsqrt(var + EPS)
    return (normed * scale + shift).astype(jnp.bfloat16)


def piece_of(count, most):
    return max(p for p in range(16, most + 1, 16) if count % p == 0)


def head_norm(values, gain):
    rms = jnp.mean(values * values, axis=-1, keepdims=True)
    return (values * lax.rsqrt(rms + EPS) * gain).astype(jnp.bfloat16)


def dot(left, right):
    return jnp.dot(left, right, preferred_element_type=jnp.float32)


def dot_t(left, right):
    return lax.dot_general(
        left, right, (((1,), (1,)), ((), ())), preferred_element_type=jnp.float32
    )


def column_step(width):
    return 2 * HD if width % (2 * HD) == 0 else HD


def softmax_rows(scores_ref, weights_ref, rate, before=None):
    count = scores_ref.shape[0]
    step = piece_of(count, 32)
    bests, totals = [], []
    for r in range(0, count, step):
        scores = scores_ref[r : r + step, :]
        best = jnp.max(scores, axis=-1, keepdims=True)
        if before is not None:
            best = jnp.maximum(best, before[r : r + step])
        weights = jnp.exp2((scores - best) * rate)
        weights_ref[r : r + step, :] = weights.astype(jnp.bfloat16)
        bests.append(best)
        totals.append(jnp.sum(weights, axis=-1, keepdims=True))
    return jnp.concatenate(bests, axis=0), jnp.concatenate(totals, axis=0)


def blocks_kernel(n_rows, n_join, left_in, attend, first, carried, last, rate, *refs):
    refs = list(refs)

    def take(count):
        taken = refs[:count]
        del refs[:count]
        return taken

    row_refs = take(n_rows)
    join_refs = take(n_join)
    mod_ref, w_ref, kg_ref = take(3)
    if first:
        (qg_ref,) = take(1)
    else:
        q_ref, left_k, left_v = take(3)
        if carried:
            state_in, acc_in = take(2)
    if last:
        (ctx_ref,) = take(1)
    else:
        if first:
            (q_ref,) = take(1)
        out_k, out_v = take(2)
        if attend:
            state_out, acc_out = take(2)
    if n_join:
        (join_ref,) = take(1)
        at = 0
        for ref in join_refs:
            join_ref[at : at + ref.shape[0], :] = ref[...]
            at += ref.shape[0]
    rows_ref, k_ref, v_ref = take(3)
    if attend:
        scores_ref, weights_ref = take(2)
    shift = mod_ref[0:1, :]
    scale = 1.0 + mod_ref[1:2, :]
    at = 0
    for ref in row_refs:
        step = piece_of(ref.shape[0], 16)
        for r in range(0, ref.shape[0], step):
            rows_ref[at : at + step, :] = modulate(ref[r : r + step, :], shift, scale)
            at += step
    if left_in:
        k_ref[:left_in, :] = left_k[...]
        v_ref[:left_in, :] = left_v[...]
    width = w_ref.shape[2]
    wide = column_step(width)
    rows = rows_ref[...]
    for c in range(0, width, wide):
        span = slice(c, c + wide)
        k_wide = dot(rows, w_ref[1, :, span])
        v_ref[left_in:, span] = dot(rows, w_ref[2, :, span]).astype(jnp.bfloat16)
        if first:
            q_wide = dot(rows, w_ref[0, :, span])
        for j in range(0, wide, HD):
            h = (c + j) // HD
            lanes = slice(c + j, c + j + HD)
            k_ref[left_in:, lanes] = head_norm(k_wide[:, j : j + HD], kg_ref[...])
            if first:
                q_ref[:, lanes] = head_norm(q_wide[:, j : j + HD], qg_ref[...])
            if not attend:
                continue
            slot = h % 2
            scores_ref[slot] = dot_t(q_ref[:, lanes], k_ref[:attend, lanes])
            before = state_in[:, 2 * h : 2 * h + 1] if carried else None
            best, total = softmax_rows(
                scores_ref.at[slot], weights_ref.at[slot], rate, before
            )
            accum = dot(weights_ref[slot], v_ref[:attend, lanes])
            if carried:
                factor = jnp.exp2((before - best) * rate)
                total = total + factor * state_in[:, 2 * h + 1 : 2 * h + 2]
                accum = accum + factor * acc_in[:, lanes]
            if last:
                ctx_ref[:, lanes] = (accum / total).astype(jnp.bfloat16)
            else:
                state_out[:, 2 * h : 2 * h + 1] = best
                state_out[:, 2 * h + 1 : 2 * h + 2] = total
                acc_out[:, lanes] = accum
    if not last:
        out_k[...] = k_ref[attend:, :]
        out_v[...] = v_ref[attend:, :]


def final_kernel(
    n_scene, rate,
    me_ref, ctx_ref, ctx_p_ref, own_ref, other_ref, mod_ref, wo_ref, wo_p_ref, wc_ref, cg_ref, *refs
):
    scene_refs = refs[:n_scene]
    hidden_ref, out_ref, hid_ref, keys_ref, swap_ref, scores_ref, weights_ref, wp_ref, sem = refs[
        n_scene:
    ]
    copy = pltpu.make_async_copy(wo_p_ref, wp_ref, sem)
    copy.start()
    half = own_ref.shape[0]
    width = ctx_ref.shape[1]
    model = own_ref.shape[1]
    wide = column_step(width)
    swap_ref[:half, :] = ctx_p_ref[half:, :]
    swap_ref[half:, :] = ctx_p_ref[:half, :]
    each = scene_refs[0].shape[0] // 2
    for i, ref in enumerate(scene_refs):
        keys_ref[0, i * each : (i + 1) * each, :] = ref[:each, :]
        keys_ref[1, i * each : (i + 1) * each, :] = ref[each:, :]
    mine = ctx_ref[...]
    copy.wait()
    swapped = swap_ref[...]
    for c in range(0, model, wide):
        cols = slice(c, c + wide)
        attn = dot(mine, wo_ref[:, cols]) + dot(swapped, wp_ref[:, cols])
        gated = mod_ref[2:3, cols] * attn
        own = (own_ref[:, cols].astype(jnp.float32) + gated[:half]).astype(jnp.bfloat16)
        hidden_ref[:, cols] = own
        hid_ref[:half, cols] = own
        hid_ref[half:, cols] = (
            other_ref[:, cols].astype(jnp.float32) + gated[half:]
        ).astype(jnp.bfloat16)
    rows = hid_ref[...]
    me = me_ref[0]
    at_own = pl.multiple_of(me * half, half)
    at_other = pl.multiple_of((1 - me) * half, half)
    for c in range(0, width, wide):
        q_wide = dot(rows, wc_ref[:, c : c + wide])
        for j in range(0, wide, HD):
            slot = ((c + j) // HD) % 2
            lanes = slice(c + j, c + j + HD)
            queries = head_norm(q_wide[:, j : j + HD], cg_ref[...])
            scores_ref[slot] = dot_t(queries, keys_ref[0, :, lanes])
            _, total = softmax_rows(scores_ref.at[slot], weights_ref.at[slot], rate)
            accum = dot(weights_ref[slot], keys_ref[1, :, lanes])
            result = (accum / total).astype(jnp.bfloat16)
            out_ref[pl.ds(at_own, half), lanes] = result[:half]
            out_ref[pl.ds(at_other, half), lanes] = result[half:]


VM = pl.BlockSpec(memory_space=pltpu.VMEM)
SM = pl.BlockSpec(memory_space=pltpu.SMEM)
ANY = pl.BlockSpec(memory_space=pl.ANY)
PARAMS = pltpu.CompilerParams(vmem_limit_bytes=20 * 1024 * 1024)
RATE = math.log2(math.e) / math.sqrt(HD)


def blocks_call(row_list, join, mod, w3, q_gain, k_gain, carry, last):
    first = carry is None
    model = row_list[0].shape[1]
    fresh = sum(r.shape[0] for r in row_list)
    width = w3.shape[2]
    rows_q = fresh if first else carry[0].shape[0]
    left_in = 0 if first else carry[1].shape[0]
    carried = not first and len(carry) > 3
    keys = left_in + fresh
    if last:
        attend = keys
    else:
        attend = 0 if first else keys // HD * HD
    args = list(row_list) + list(join) + [mod, w3, k_gain]
    args += [q_gain] if first else list(carry)
    half = jnp.bfloat16
    shapes = []
    if last:
        shapes.append(((rows_q, width), half))
    else:
        if first:
            shapes.append(((rows_q, width), half))
        shapes += [((keys - attend, width), half)] * 2
        if attend:
            shapes += [((rows_q, HD), jnp.float32), ((rows_q, width), jnp.float32)]
    if join:
        shapes.append(((sum(r.shape[0] for r in join), width), half))
    scratch = [
        pltpu.VMEM((fresh, model), half),
        pltpu.VMEM((keys, width), half),
        pltpu.VMEM((keys, width), half),
    ]
    if attend:
        scratch += [
            pltpu.VMEM((2, rows_q, attend), jnp.float32),
            pltpu.VMEM((2, rows_q, attend), half),
        ]
    flops = 2 * fresh * model * width * (3 if first else 2) + 4 * rows_q * attend * width
    out = pl.pallas_call(
        functools.partial(
            blocks_kernel,
            len(row_list), len(join), left_in, attend, first, carried, last, RATE,
        ),
        out_shape=[jax.ShapeDtypeStruct(*s) for s in shapes],
        in_specs=[VM] * len(args),
        out_specs=[VM] * len(shapes),
        scratch_shapes=scratch,
        compiler_params=PARAMS,
        cost_estimate=pl.CostEstimate(
            flops=flops,
            transcendentals=rows_q * attend * width // HD,
            bytes_accessed=2 * fresh * model + 6 * model * width,
        ),
    )(*args)
    out = list(out)
    joined = out.pop() if join else None
    if last:
        return out[0], joined
    return (tuple(out) if first else (carry[0],) + tuple(out)), joined


def final_call(me, ctx, ctx_p, own, other, mod, wo, wo_p, wc, cg, scenes):
    half, model = own.shape
    rows, width = ctx.shape
    each = scenes[0].shape[0] // 2
    keys = each * len(scenes)
    args = [me, ctx, ctx_p, own, other, mod, wo, wo_p, wc, cg] + list(scenes)
    flops = 4 * rows * model * width + 2 * rows * model * width
    return pl.pallas_call(
        functools.partial(final_kernel, len(scenes), RATE),
        out_shape=[
            jax.ShapeDtypeStruct((half, model), jnp.bfloat16),
            jax.ShapeDtypeStruct((rows, width), jnp.bfloat16),
        ],
        in_specs=[SM] + [VM] * 6 + [ANY] + [VM] * (len(args) - 8),
        out_specs=[VM, VM],
        scratch_shapes=[
            pltpu.VMEM((rows, model), jnp.bfloat16),
            pltpu.VMEM((2, keys, width), jnp.bfloat16),
            pltpu.VMEM((rows, width), jnp.bfloat16),
            pltpu.VMEM((2, rows, keys), jnp.float32),
            pltpu.VMEM((2, rows, keys), jnp.bfloat16),
            pltpu.VMEM(wo_p.shape, jnp.bfloat16),
            pltpu.SemaphoreType.DMA(()),
        ],
        compiler_params=PARAMS,
        cost_estimate=pl.CostEstimate(
            flops=flops,
            transcendentals=rows * keys * width // HD,
            bytes_accessed=6 * model * width,
        ),
        name="final",
    )(*args)


def swap_cores(x):
    return lax.ppermute(x, "head", [(0, 1), (1, 0)])


def blk_permute(x, pairs):
    return lax.ppermute(x, "blk", pairs)


def body(
    tokens, modulation, w_qkv, w_out, w_cross, q_gain, k_gain, cross_gain, scene_keys, scene_values
):
    count = lax.axis_size("blk")
    me = lax.axis_index("head").astype(jnp.int32).reshape(1)
    place = lax.axis_index("blk")
    w3 = jnp.transpose(w_qkv, (1, 0, 2))
    q_gain, k_gain, cross_gain = (g.reshape(1, HD) for g in (q_gain, k_gain, cross_gain))
    other = swap_cores(tokens)
    w_out_p = swap_cores(w_out)
    at_end = (place == 0) | (place == count - 1)

    def gather(x):
        if count != 4:
            return [
                blk_permute(x, [(i, (i + s) % count) for i in range(count)])
                for s in range(1, count)
            ]
        near = blk_permute(x, [(i, i ^ 1) for i in range(4)])
        far = blk_permute(x, [(i, i ^ 2) for i in range(4)])
        mid = blk_permute(x, [(1, 2), (2, 1)])
        out = blk_permute(far, [(1, 0), (2, 3)])
        return [near, far, jnp.where(at_end, out, mid)]

    slots = gather(tokens)
    carry, scene = blocks_call(
        [tokens, other], [scene_keys, scene_values], modulation, w3, q_gain, k_gain,
        None, count == 1,
    )
    scenes = [scene] + gather(scene)
    pairs = [(x, swap_cores(x)) for x in slots]
    while pairs:
        taken, pairs = (pairs[:2], pairs[2:]) if len(pairs) > 1 else (pairs, [])
        carry, _ = blocks_call(
            [r for pair in taken for r in pair], [],
            modulation, w3, q_gain, k_gain, carry, not pairs,
        )
    ctx = carry
    ctx_p = swap_cores(ctx)
    hidden, cross_context = final_call(
        me, ctx, ctx_p, tokens, other, modulation, w_out, w_out_p, w_cross, cross_gain, scenes
    )
    return (hidden, cross_context)


def solution(mesh):
    return jax.shard_map(
        body,
        mesh=mesh,
        in_specs=(
            P(("clip", "blk", "head"), None),
            P("clip", None),
            P(None, None, "head"),
            P("head", None),
            P(None, "head"),
            P(),
            P(),
            P(),
            P(("clip", "blk"), "head"),
            P(("clip", "blk"), "head"),
        ),
        out_specs=(P(("clip", "blk", "head"), None), P(("clip", "blk"), "head")),
        check_vma=False,
    )
```
